512 devices in a mesh: pipe: 16 (over z_hi, x), dp: 32 (over y, z_lo, core).
Axes of the slice: x: 4, y: 8, z: 8 (z_hi: 4, z_lo: 2; z = z_hi * 2 + z_lo), core: 2. Of those that a mesh axis runs over, the one named last changes fastest.
Arguments:
- activations: bfloat16 [2, 16, 4096, 6144], P(None, 'pipe', 'dp'), may hold values from -6 to 6
- queries: bfloat16 [2, 16, 4096, 128], P(None, 'pipe', 'dp'), may hold values from -16 to 16
- keys: bfloat16 [2, 16, 4096, 128], P(None, 'pipe', 'dp'), may hold values from -16 to 16
- grad_out: bfloat16 [2, 16, 4096, 128], P(None, 'pipe', 'dp'), may hold values from -0.4375 to 0.4375
- segment_ids: int32 [2, 16, 32, 128], P(None, 'pipe', 'dp'), may hold values from 0 to 3, never falling along the last dimension, each value on 1 to 64 neighbouring positions
Outputs:
- grad_value: bfloat16 [16, 6144, 128], P('pipe', 'dp')
The draws below stay inside these ranges and needn't reach their ends.
Inputs may be any that keep to these rules, and one draw needn't show every extreme that they name: `segment_ids`: ids restart at 0 in every micro-batch; each document spans 1 to 64 tokens, one exactly that many.
All inputs are finite; a program needn't handle non-finite values.
Results may differ from the reference program's by a relative error of at most 0.0063.
Values sent between devices are 32-bit elements; how exact they have to be, the bound alone decides.
A program may use at most 64 MiB of HBM per device.

```python
import math
import jax
import jax.numpy as jnp
import numpy as np
from jax import lax

D = 6144
HEAD = 128
MB_LEN = 128
DOCS = 4
SECTIONS = 16
TOKENS = 4096
N_DP = 32


def query_key_pair(key):
    base_key = jax.random.fold_in(key, 4242)
    query_key, key_key = jax.random.split(base_key, 2)
    shape = (2, SECTIONS, TOKENS, HEAD)
    query_draw = jnp.clip(jax.random.normal(query_key, shape, jnp.float32), -6.0, 6.0)
    key_draw = jnp.clip(jax.random.normal(key_key, shape, jnp.float32), -6.0, 6.0)
    return (query_draw, key_draw)


def draw_queries(key, part):
    return query_key_pair(key)[0].astype(jnp.bfloat16)


def draw_keys(key, part):
    return query_key_pair(key)[1].astype(jnp.bfloat16)


def with_spikes(result, stream_key, source, target, blocks, factor):
    def block_of(dim):
        return (jnp.arange(result.shape[dim]) // (result.shape[dim] // blocks)).reshape((-1,) + (1,) * (result.ndim - 1 - dim))

    one_side = jax.random.permutation(stream_key, blocks)[block_of(target)]
    second = (block_of(target) + blocks // 2) % blocks
    return jnp.where((block_of(source) == one_side) | (block_of(source) == second), factor * result, result)


def block_scale(stream_key, dims, shards, least, top_value):
    gain, own = 1.0, jax.random.fold_in(stream_key, 6)
    for dim, shards_of in shards:
        steps = jnp.exp(jax.random.uniform(jax.random.fold_in(own, dim), (shards_of,), jnp.float32, least / len(shards), top_value / len(shards)))
        gain = gain * jnp.repeat(steps, dims[dim] // shards_of).reshape([-1 if axis == dim else 1 for axis in range(len(dims))])
    return gain


def profile(number_of, total, bound, slope):
    weights = [(1 << 20) // math.isqrt(standing ** slope) + 1 for standing in range(2, number_of + 1)]
    spare, counts = total - bound - (number_of - 1), [1] * (number_of - 1)
    while spare > 0:
        candidates = [i for i in range(number_of - 1) if counts[i] < bound]
        pool, left = sum([weights[i] for i in candidates]), spare
        for i in candidates:
            addition = min(bound - counts[i], max(1, left * weights[i] // pool), spare)
            counts[i] = counts[i] + addition
            spare = spare - addition
    return np.array([bound] + counts)


def ragged_sizes(stream_key, count, total, bound, skew):
    if count == 2:
        one = jax.random.randint(stream_key, (), max(1, total - bound), min(bound, total - 1) + 1)
        return jnp.stack([one, total - one])
    tallies = jnp.asarray(profile(count, total, bound, skew), jnp.int32)
    couples = (count - 1) // 2
    giver, taker = tallies[1:1 + 2 * couples:2], tallies[2:2 + 2 * couples:2]
    room = jnp.minimum(giver - 1, bound - taker)
    moved = jax.random.randint(jax.random.fold_in(stream_key, 1), (couples,), 0, 1 << 20) % (room + 1)
    tallies = tallies.at[1:1 + 2 * couples:2].set(giver - moved).at[2:2 + 2 * couples:2].set(taker + moved)
    return tallies[jax.random.permutation(jax.random.fold_in(stream_key, 2), count)]


def normal_values(key, extent, deviation, bound, cuts=(), held_as=jnp.bfloat16):
    factor_of = block_scale(key, extent, cuts, -0.22, 0.18) if cuts else 1.0
    result = jax.random.normal(key, extent, jnp.float32) * deviation * factor_of
    return jnp.minimum(jnp.maximum(result, -bound), bound).astype(held_as)


def heavy_noise(own_key, dims, width, bound, pieces, heavy, kind=jnp.bfloat16):
    values = width * jax.random.normal(own_key, dims, jnp.float32)
    if pieces:
        values = values * block_scale(own_key, dims, pieces, -0.22, 0.18)
    return jnp.clip(with_spikes(values, jax.random.fold_in(own_key, 3), *heavy), -bound, bound).astype(kind)


def setup_inputs(seed: int = 0) -> dict:
    splits = jax.random.split(jax.random.key(seed), 6)
    activations = heavy_noise(splits[0], (2, SECTIONS, TOKENS, D), 1.0, 6.0, ((1, 16), (2, 32)), (2, 3, 32, 2.75))
    queries = draw_queries(jax.random.fold_in(splits[5], 71), 0)
    keys = draw_keys(jax.random.fold_in(splits[5], 71), 0)
    grad_out = normal_values(splits[3], (2, SECTIONS, TOKENS, HEAD), 0.03, 0.4375, ((1, 16), (2, 32)))
    segment_ids = jax.vmap(lambda own: jnp.searchsorted(jnp.cumsum(ragged_sizes(own, DOCS, MB_LEN, MB_LEN // 2, 2)), jnp.arange(MB_LEN), side="right"))(jax.random.split(splits[4], 2 * SECTIONS * N_DP)).reshape((2, SECTIONS, N_DP, MB_LEN)).astype(jnp.int32)
    return {"activations": activations, "queries": queries, "keys": keys, "grad_out": grad_out, "segment_ids": segment_ids}


def replica_partial(acts, query_rows, key_rows, grad_rows, segs):
    scores = jnp.dot(query_rows, key_rows.T, preferred_element_type=jnp.float32) / jnp.sqrt(jnp.float32(HEAD))
    position = jnp.arange(MB_LEN, dtype=jnp.int32)
    keep = (position[None, :] <= position[:, None]) & (segs[None, :] == segs[:, None])
    masked = jnp.where(keep, scores, jnp.float32(-1e+30))
    top = lax.optimization_barrier(jnp.max(masked, axis=1, keepdims=True))
    weights = jnp.where(keep, jnp.exp(masked - top), jnp.float32(0.0))
    probs = (weights / lax.optimization_barrier(jnp.sum(weights, axis=1, keepdims=True))).astype(jnp.bfloat16)
    probs = lax.optimization_barrier(probs)
    grad_v = jnp.einsum('qk,qd->kd', probs.astype(jnp.float32), grad_rows.astype(jnp.float32)).astype(jnp.bfloat16)
    grad_v = lax.optimization_barrier(grad_v)
    partial_value = jnp.einsum('td,te->de', acts.astype(jnp.float32), grad_v.astype(jnp.float32)).astype(jnp.bfloat16)
    return lax.optimization_barrier(partial_value)

def slot_sum(items):
    acts, query_rows, key_rows, grad_rows, segs = items
    parts = jax.vmap(replica_partial)(acts.reshape(N_DP, MB_LEN, D), query_rows.reshape(N_DP, MB_LEN, HEAD), key_rows.reshape(N_DP, MB_LEN, HEAD), grad_rows.reshape(N_DP, MB_LEN, HEAD), segs)
    return lax.optimization_barrier(jnp.sum(parts.astype(jnp.float32), axis=0))

def reference(activations, queries, keys, grad_out, segment_ids):
    count = 2 * SECTIONS
    sums = lax.map(slot_sum, (activations.reshape(count, TOKENS, D), queries.reshape(count, TOKENS, HEAD), keys.reshape(count, TOKENS, HEAD), grad_out.reshape(count, TOKENS, HEAD), segment_ids.reshape(count, N_DP, MB_LEN)))
    sums = sums.reshape(2, SECTIONS, D, HEAD)
    total = sums[0] + sums[1][::-1]
    return total.astype(jnp.bfloat16)
```

```python
import functools

import jax
import jax.numpy as jnp
from jax import lax
from jax.experimental import pallas as pl
from jax.experimental.pallas import tpu as pltpu
from jax.sharding import PartitionSpec as P

MESH = pl.DeviceIdType.MESH
RING = 8
OFFSETS = (4, 3, -3, 2, -2, 1, -1, 0)
SLOTS = len(OFFSETS)
PLUS = {2: 1, 3: 3, 4: 5}
MINUS = {2: 2, 3: 4, 4: 6}


def transposed_dot(a, b):
    return lax.dot_general(a, b, (((0,), (0,)), ((), ())), preferred_element_type=jnp.float32)


def head_gradient(query_rows, key_rows, grad_rows, segs):
    length, head = query_rows.shape
    scores = lax.dot_general(
        query_rows, key_rows, (((1,), (1,)), ((), ())), preferred_element_type=jnp.float32
    ) / jnp.sqrt(jnp.float32(head))
    across = jnp.broadcast_to(segs.astype(jnp.float32), (length, length))
    down = across.T
    row = lax.broadcasted_iota(jnp.int32, (length, length), 0)
    column = lax.broadcasted_iota(jnp.int32, (length, length), 1)
    keep = (column <= row) & (across == down)
    masked = jnp.where(keep, scores, jnp.float32(-1e30))
    top = jnp.max(masked, axis=1, keepdims=True)
    weights = jnp.where(keep, jnp.exp(masked - top), jnp.float32(0.0))
    probs = (weights / jnp.sum(weights, axis=1, keepdims=True)).astype(jnp.bfloat16)
    return transposed_dot(probs, grad_rows).astype(jnp.bfloat16)


def kernel(
    split, pipes, acts, queries, keys, grads, segs, out,
    q_buf, k_buf, g_buf, s_buf, a_buf, head_grad,
    part, twin, pair, y_first, y_rest, z_first, z_rest, y_tail, z_tail, total,
    load_sem, x_send, x_recv, p_send, p_recv, y_send, y_recv, z_send, z_recv, t_send, t_recv,
):
    pipe, dp = lax.axis_index("pipe"), lax.axis_index("dp")
    y, low, core = dp // 4, (dp // 2) % 2, dp % 2
    rows = out.shape[0]

    def at(pipe_index, y_index, low_index, core_index):
        return {"pipe": pipe_index, "dp": y_index * 4 + low_index * 2 + core_index}

    twin_id = at(pipe, y, low, 1 - core)
    pair_id = at(pipe, y, 1 - low, core)
    plus_id = at(pipe, (y + 1) % RING, low, core)
    minus_id = at(pipe, (y + RING - 1) % RING, low, core)
    mirror_id = at(pipes - 1 - pipe, y, low, core)
    across_id = at(pipes - 1 - pipe, y, 1 - low, core)
    peers = (twin_id, pair_id, plus_id, minus_id, mirror_id, across_id)

    barrier = pltpu.get_barrier_semaphore()
    for peer in peers:
        pl.semaphore_signal(barrier, inc=1, device_id=peer, device_id_type=MESH)

    def load(src, dst, number):
        copy = pltpu.make_async_copy(src, dst, load_sem.at[number])
        copy.start()
        return copy

    small = [
        load(src, dst, number)
        for number, (src, dst) in enumerate(
            ((queries, q_buf), (keys, k_buf), (grads, g_buf), (segs, s_buf))
        )
    ]
    wide = 4 * rows
    large = []
    for slot, offset in enumerate(OFFSETS):
        first = pl.multiple_of(((y + RING + offset) % RING) * wide, 128)
        large.append(load(acts.at[:, :, pl.ds(first, wide)], a_buf.at[slot], 4 + slot))
    for copy in small:
        copy.wait()
    for half in range(2):
        head_grad[half] = head_gradient(q_buf[half], k_buf[half], g_buf[half], s_buf[half])

    started = []

    def send(src, dst, send_sem, recv_sem, peer):
        copy = pltpu.make_async_remote_copy(
            src_ref=src, dst_ref=dst, send_sem=send_sem, recv_sem=recv_sem,
            device_id=peer, device_id_type=MESH,
        )
        copy.start()
        started.append(copy)
        return copy

    def product(slot):
        large[slot].wait()
        for half in range(2):
            block = transposed_dot(a_buf[slot, half], head_grad[half])
            for z in range(2):
                for c in range(2):
                    start = (z * 2 + c) * rows
                    part[slot, c, half, z] = block[start : start + rows]

    exchanges, pairs = [], []

    def trade(slot):
        exchanges.append(
            send(part.at[slot, 1 - core], twin.at[slot], x_send.at[slot], x_recv.at[slot], twin_id)
        )

    def merge(slot):
        exchanges[slot].wait_recv()
        part[slot, core] += twin[slot]
        pairs.append(
            send(
                part.at[slot, core, :, 1 - low, split:], pair.at[slot],
                p_send.at[slot], p_recv.at[slot], pair_id,
            )
        )

    def settle(slot):
        pairs[slot].wait_recv()
        part[slot, core, :, low, split:] += pair[slot]

    ways = (plus_id, minus_id)
    y_copies, z_copies = {}, {}

    def y_start():
        for way in range(2):
            y_copies[1, way] = send(
                part.at[0, core, way, :, :split], y_first.at[way],
                y_send.at[way], y_recv.at[way], ways[way],
            )

    def z_start():
        for way in range(2):
            z_copies[1, way] = send(
                part.at[0, core, way, low, split:], z_first.at[way],
                z_send.at[way], z_recv.at[way], ways[way],
            )

    def y_arrive(step, way, slot):
        y_copies[step, way].wait_recv()
        if step == 1:
            part[slot, core, way, :, :split] += y_first[way]
        else:
            part[slot, core, :, :, :split] += y_rest[way, step - 2]

    def z_arrive(step, way, slot):
        z_copies[step, way].wait_recv()
        if step == 1:
            part[slot, core, way, low, split:] += z_first[way]
        else:
            part[slot, core, :, low, split:] += z_rest[way, step - 2]

    def y_step(step):
        for way, slot in ((0, PLUS[step]), (1, MINUS[step])):
            y_arrive(step - 1, way, slot)
            number = 2 * (step - 1) + way
            y_copies[step, way] = send(
                part.at[slot, core, :, :, :split], y_rest.at[way, step - 2],
                y_send.at[number], y_recv.at[number], ways[way],
            )

    def z_step(step):
        for way, slot in ((0, PLUS[step]), (1, MINUS[step])):
            settle(slot)
            z_arrive(step - 1, way, slot)
            number = 2 * (step - 1) + way
            z_copies[step, way] = send(
                part.at[slot, core, :, low, split:], z_rest.at[way, step - 2],
                z_send.at[number], z_recv.at[number], ways[way],
            )

    last = SLOTS - 1
    for slot in range(SLOTS):
        product(slot)
        if slot == 0:
            pl.semaphore_wait(barrier, len(peers))
        trade(slot)
        if slot >= 2:
            merge(slot - 2)
        if slot == 2:
            y_start()
    merge(last - 1)
    merge(last)
    settle(0)
    z_start()
    for step in (2, 3, 4):
        y_step(step)
        z_step(step)

    tails = []
    for way in range(2):
        y_arrive(4, way, last)
    for number, (half, z, peer) in enumerate(
        ((1, 1 - low, across_id), (1, low, mirror_id), (0, 1 - low, pair_id))
    ):
        tails.append(
            send(
                part.at[last, core, half, z, :split], y_tail.at[number],
                t_send.at[number], t_recv.at[number], peer,
            )
        )
    settle(last)
    for way in range(2):
        z_arrive(4, way, last)
    tails.append(
        send(part.at[last, core, 1, low, split:], z_tail, t_send.at[3], t_recv.at[3], mirror_id)
    )
    for copy in tails:
        copy.wait_recv()
    total[:split] = part[last, core, 0, low, :split] + y_tail[0] + y_tail[1] + y_tail[2]
    total[split:] = part[last, core, 0, low, split:] + z_tail[...]
    out[...] = total[...].astype(out.dtype)
    for copy in started:
        copy.wait_send()


def body(activations, queries, keys, grad_out, segment_ids):
    _, _, length, width = activations.shape
    head = queries.shape[-1]
    count, pipes = lax.axis_size("dp"), lax.axis_size("pipe")
    rows = width // count
    split = rows * 5 // 12 // 8 * 8
    rest = rows - split
    f32, bf16 = jnp.float32, jnp.bfloat16
    dma = lambda *shape: pltpu.SemaphoreType.DMA(shape)
    result = pl.pallas_call(
        functools.partial(kernel, split, pipes),
        out_shape=jax.ShapeDtypeStruct((rows, head), bf16),
        in_specs=[pl.BlockSpec(memory_space=pl.ANY)] * 5,
        out_specs=pl.BlockSpec(memory_space=pltpu.VMEM),
        scratch_shapes=[
            pltpu.VMEM((2, length, head), bf16),
            pltpu.VMEM((2, length, head), bf16),
            pltpu.VMEM((2, length, head), bf16),
            pltpu.VMEM((2, 1, length), jnp.int32),
            pltpu.VMEM((SLOTS, 2, length, 4 * rows), bf16),
            pltpu.VMEM((2, length, head), bf16),
            pltpu.VMEM((SLOTS, 2, 2, 2, rows, head), f32),
            pltpu.VMEM((SLOTS, 2, 2, rows, head), f32),
            pltpu.VMEM((SLOTS, 2, rest, head), f32),
            pltpu.VMEM((2, 2, split, head), f32),
            pltpu.VMEM((2, 3, 2, 2, split, head), f32),
            pltpu.VMEM((2, rest, head), f32),
            pltpu.VMEM((2, 3, 2, rest, head), f32),
            pltpu.VMEM((3, split, head), f32),
            pltpu.VMEM((rest, head), f32),
            pltpu.VMEM((rows, head), f32),
            dma(12), dma(SLOTS), dma(SLOTS), dma(SLOTS), dma(SLOTS),
            dma(8), dma(8), dma(8), dma(8), dma(4), dma(4),
        ],
        compiler_params=pltpu.CompilerParams(
            collective_id=0, has_side_effects=True, vmem_limit_bytes=48 * 2**20
        ),
        name="reduce_value_grad",
    )(
        activations.reshape(2, length, width),
        queries.reshape(2, length, head),
        keys.reshape(2, length, head),
        grad_out.reshape(2, length, head),
        segment_ids.reshape(2, 1, length),
    )
    return result[None]


def solution(mesh):
    return jax.shard_map(
        body,
        mesh=mesh,
        in_specs=(
            P(None, "pipe", "dp", None),
            P(None, "pipe", "dp", None),
            P(None, "pipe", "dp", None),
            P(None, "pipe", "dp", None),
            P(None, "pipe", "dp", None),
        ),
        out_specs=P("pipe", "dp", None),
        check_vma=False,
    )
```

```python
import functools

import jax
import jax.numpy as jnp
from jax import lax
from jax.experimental import pallas as pl
from jax.experimental.pallas import tpu as pltpu
from jax.sharding import PartitionSpec as P

MESH = pl.DeviceIdType.MESH
RING = 8
OFFSETS = (4, 3, -3, 2, -2, 1, -1, 0)
SLOTS = len(OFFSETS)
PLUS = {2: 1, 3: 3, 4: 5}
MINUS = {2: 2, 3: 4, 4: 6}


def transposed_dot(a, b):
    return lax.dot_general(a, b, (((0,), (0,)), ((), ())), preferred_element_type=jnp.float32)


def head_gradient(query_rows, key_rows, grad_rows, segs):
    length, head = query_rows.shape
    scores = lax.dot_general(
        query_rows, key_rows, (((1,), (1,)), ((), ())), preferred_element_type=jnp.float32
    ) / jnp.sqrt(jnp.float32(head))
    across = jnp.broadcast_to(segs.astype(jnp.float32), (length, length))
    down = across.T
    row = lax.broadcasted_iota(jnp.int32, (length, length), 0)
    column = lax.broadcasted_iota(jnp.int32, (length, length), 1)
    keep = (column <= row) & (across == down)
    masked = jnp.where(keep, scores, jnp.float32(-1e30))
    top = jnp.max(masked, axis=1, keepdims=True)
    weights = jnp.where(keep, jnp.exp(masked - top), jnp.float32(0.0))
    probs = (weights / jnp.sum(weights, axis=1, keepdims=True)).astype(jnp.bfloat16)
    return transposed_dot(probs, grad_rows).astype(jnp.bfloat16)


def kernel(
    split, pipes, acts, queries, keys, grads, segs, out,
    q_buf, k_buf, g_buf, s_buf, a_buf, head_grad,
    part, twin, pair, y_first, y_rest, z_first, z_rest, y_tail, z_tail, total,
    load_sem, x_send, x_recv, p_send, p_recv, y_send, y_recv, z_send, z_recv, t_send, t_recv,
    far_sem,
):
    pipe, dp = lax.axis_index("pipe"), lax.axis_index("dp")
    y, low, core = dp // 4, (dp // 2) % 2, dp % 2
    rows = out.shape[0]
    rest = rows - split

    def at(pipe_index, y_index, low_index, core_index):
        return {"pipe": pipe_index, "dp": y_index * 4 + low_index * 2 + core_index}

    twin_id = at(pipe, y, low, 1 - core)
    pair_id = at(pipe, y, 1 - low, core)
    plus_id = at(pipe, (y + 1) % RING, low, core)
    minus_id = at(pipe, (y + RING - 1) % RING, low, core)
    mirror_id = at(pipes - 1 - pipe, y, low, core)
    across_id = at(pipes - 1 - pipe, y, 1 - low, core)
    near = (twin_id, pair_id, plus_id, minus_id)
    distant = (mirror_id, across_id)
    upper = pipe // (pipes // 2)

    barrier = pltpu.get_barrier_semaphore()
    for peer in near:
        pl.semaphore_signal(barrier, inc=1, device_id=peer, device_id_type=MESH)

    @pl.when(upper == 0)
    def _():
        for peer in distant:
            pl.semaphore_signal(barrier, inc=1, device_id=peer, device_id_type=MESH)

    def meet():
        pl.semaphore_wait(barrier, len(near) + len(distant) * upper)

        @pl.when(upper == 1)
        def _():
            for peer in distant:
                pl.semaphore_signal(far_sem, inc=1, device_id=peer, device_id_type=MESH)

    def meet_distant():
        @pl.when(upper == 0)
        def _():
            pl.semaphore_wait(far_sem, len(distant))

    def load(src, dst, number):
        copy = pltpu.make_async_copy(src, dst, load_sem.at[number])
        copy.start()
        return copy

    small = [
        load(src, dst, number)
        for number, (src, dst) in enumerate(
            ((queries, q_buf), (keys, k_buf), (grads, g_buf), (segs, s_buf))
        )
    ]
    wide = 4 * rows
    large = []
    for slot, offset in enumerate(OFFSETS):
        first = pl.multiple_of(((y + RING + offset) % RING) * wide, 128)
        large.append(load(acts.at[:, :, pl.ds(first, wide)], a_buf.at[slot], 4 + slot))
    for copy in small:
        copy.wait()
    for half in (1, 0):
        head_grad[half] = head_gradient(q_buf[half], k_buf[half], g_buf[half], s_buf[half])

    started = []

    def send(src, dst, send_sem, recv_sem, peer):
        copy = pltpu.make_async_remote_copy(
            src_ref=src, dst_ref=dst, send_sem=send_sem, recv_sem=recv_sem,
            device_id=peer, device_id_type=MESH,
        )
        copy.start()
        started.append(copy)
        return copy

    loaded, exchanges, pairs, y_copies, z_copies, tails = set(), {}, {}, {}, {}, {}
    ways = (plus_id, minus_id)
    last = SLOTS - 1

    def product(half, *slots):
        for slot in slots:
            if slot not in loaded:
                loaded.add(slot)
                large[slot].wait()
            block = transposed_dot(a_buf[slot, half], head_grad[half])
            for z in range(2):
                for c in range(2):
                    start = (z * 2 + c) * rows
                    part[slot, c, half, z] = block[start : start + rows]
            if not exchanges:
                meet()
            number = 2 * slot + half
            exchanges[slot, half] = send(
                part.at[slot, 1 - core, half], twin.at[slot, half],
                x_send.at[number], x_recv.at[number], twin_id,
            )

    def merge(half, *slots):
        for slot in slots:
            exchanges[slot, half].wait_recv()
            part[slot, core, half] += twin[slot, half]

    def halve(half, *slots):
        for slot in slots:
            number = 2 * slot + half
            pairs[slot, half] = send(
                part.at[slot, core, half, 1 - low, split:], pair.at[slot, half],
                p_send.at[number], p_recv.at[number], pair_id,
            )

    def settle(half, slot):
        pairs[slot, half].wait_recv()
        part[slot, core, half, low, split:] += pair[slot, half]

    def y_arrive(half, step, way, slot):
        y_copies[half, step, way].wait_recv()
        if step == 1:
            part[slot, core, half, way, :split] += y_first[half, way]
        else:
            part[slot, core, half, :, :split] += y_rest[half, way, step - 2]

    def z_span(way):
        return slice(split + way * (rest // 2), split + (way + 1) * (rest // 2))

    def z_arrive(half, step, way, slot):
        z_copies[half, step, way].wait_recv()
        if step == 1:
            part[slot, core, half, low, z_span(way)] += z_first[half, way]
        else:
            part[slot, core, half, low, split:] += z_rest[half, way, step - 2]

    def y_step(half, step):
        for way in range(2):
            if step == 1:
                src, dst = part.at[0, core, half, way, :split], y_first.at[half, way]
            else:
                slot = (PLUS, MINUS)[way][step]
                y_arrive(half, step - 1, way, slot)
                src, dst = part.at[slot, core, half, :, :split], y_rest.at[half, way, step - 2]
            number = (half * 4 + step - 1) * 2 + way
            y_copies[half, step, way] = send(
                src, dst, y_send.at[number], y_recv.at[number], ways[way]
            )

    def z_step(half, step):
        if step == 1:
            settle(half, 0)
        for way in range(2):
            if step == 1:
                src, dst = part.at[0, core, half, low, z_span(way)], z_first.at[half, way]
            else:
                slot = (PLUS, MINUS)[way][step]
                settle(half, slot)
                z_arrive(half, step - 1, way, slot)
                src, dst = part.at[slot, core, half, low, split:], z_rest.at[half, way, step - 2]
            number = (half * 4 + step - 1) * 2 + way
            z_copies[half, step, way] = send(
                src, dst, z_send.at[number], z_recv.at[number], ways[way]
            )

    def y_end(half):
        for way in range(2):
            y_arrive(half, 4, way, last)
        goals = ((1 - low, across_id), (low, mirror_id)) if half else ((1 - low, pair_id),)
        for number, (z, peer) in enumerate(goals, 0 if half else 2):
            tails[number] = send(
                part.at[last, core, half, z, :split], y_tail.at[number],
                t_send.at[number], t_recv.at[number], peer,
            )

    def z_end(half):
        settle(half, last)
        for way in range(2):
            z_arrive(half, 4, way, last)
        if half:
            tails[3] = send(
                part.at[last, core, half, low, split:], z_tail,
                t_send.at[3], t_recv.at[3], mirror_id,
            )

    product(1, 0)
    product(0, 0)
    product(1, 1, 2)
    merge(1, 0)
    halve(1, 0)
    y_step(1, 1)
    product(0, 1, 2)
    merge(0, 0)
    y_step(0, 1)
    product(1, 3, 4)
    merge(1, 1, 2)
    halve(1, 1, 2)
    product(0, 3, 4)
    merge(0, 1, 2)
    y_step(1, 2)
    product(1, 5, 6, 7)
    merge(1, 3, 4)
    halve(1, 3, 4)
    z_step(1, 1)
    product(0, 5, 6, 7)
    y_step(0, 2)
    merge(1, 5, 6, 7)
    halve(1, 5, 6, 7)
    merge(0, 3, 4, 5, 6, 7)
    halve(0, 0, 1, 2, 3, 4, 5, 6, 7)
    z_step(1, 2)
    y_step(1, 3)
    y_step(0, 3)
    z_step(1, 3)
    y_step(1, 4)
    z_step(1, 4)
    y_step(0, 4)
    z_step(0, 1)
    meet_distant()
    y_end(1)
    z_end(1)
    z_step(0, 2)
    y_end(0)
    z_step(0, 3)
    z_step(0, 4)
    z_end(0)
    for number in sorted(tails):
        tails[number].wait_recv()
    total[:split] = part[last, core, 0, low, :split] + y_tail[0] + y_tail[1] + y_tail[2]
    total[split:] = part[last, core, 0, low, split:] + z_tail[...]
    out[...] = total[...].astype(out.dtype)
    for copy in started:
        copy.wait_send()


def body(activations, queries, keys, grad_out, segment_ids):
    _, _, length, width = activations.shape
    head = queries.shape[-1]
    count, pipes = lax.axis_size("dp"), lax.axis_size("pipe")
    rows = width // count
    split = rows // 2
    rest = rows - split
    f32, bf16 = jnp.float32, jnp.bfloat16
    dma = lambda *shape: pltpu.SemaphoreType.DMA(shape)
    result = pl.pallas_call(
        functools.partial(kernel, split, pipes),
        out_shape=jax.ShapeDtypeStruct((rows, head), bf16),
        in_specs=[pl.BlockSpec(memory_space=pltpu.HBM)] * 5,
        out_specs=pl.BlockSpec(memory_space=pltpu.VMEM),
        scratch_shapes=[
            pltpu.VMEM((2, length, head), bf16),
            pltpu.VMEM((2, length, head), bf16),
            pltpu.VMEM((2, length, head), bf16),
            pltpu.VMEM((2, 1, length), jnp.int32),
            pltpu.VMEM((SLOTS, 2, length, 4 * rows), bf16),
            pltpu.VMEM((2, length, head), bf16),
            pltpu.VMEM((SLOTS, 2, 2, 2, rows, head), f32),
            pltpu.VMEM((SLOTS, 2, 2, rows, head), f32),
            pltpu.VMEM((SLOTS, 2, rest, head), f32),
            pltpu.VMEM((2, 2, split, head), f32),
            pltpu.VMEM((2, 2, 3, 2, split, head), f32),
            pltpu.VMEM((2, 2, rest // 2, head), f32),
            pltpu.VMEM((2, 2, 3, rest, head), f32),
            pltpu.VMEM((3, split, head), f32),
            pltpu.VMEM((rest, head), f32),
            pltpu.VMEM((rows, head), f32),
            dma(4 + SLOTS), dma(2 * SLOTS), dma(2 * SLOTS), dma(2 * SLOTS), dma(2 * SLOTS),
            dma(16), dma(16), dma(16), dma(16), dma(4), dma(4), pltpu.SemaphoreType.REGULAR,
        ],
        compiler_params=pltpu.CompilerParams(
            collective_id=0, has_side_effects=True, vmem_limit_bytes=67_043_328
        ),
        name="reduce_value_grad",
    )(
        activations.reshape(2, length, width),
        queries.reshape(2, length, head),
        keys.reshape(2, length, head),
        grad_out.reshape(2, length, head),
        segment_ids.reshape(2, 1, length),
    )
    return result[None]


def solution(mesh):
    return jax.shard_map(
        body,
        mesh=mesh,
        in_specs=(
            P(None, "pipe", "dp", None),
            P(None, "pipe", "dp", None),
            P(None, "pipe", "dp", None),
            P(None, "pipe", "dp", None),
            P(None, "pipe", "dp", None),
        ),
        out_specs=P("pipe", "dp", None),
        check_vma=False,
    )
```

```python
import functools

import jax
import jax.numpy as jnp
from jax import lax
from jax.experimental import pallas as pl
from jax.experimental.pallas import tpu as pltpu
from jax.sharding import PartitionSpec as P

MESH = pl.DeviceIdType.MESH
RING = 8
OFFSETS = (4, 3, -3, 2, -2, 1, -1, 0)
SLOTS = len(OFFSETS)
GROUPS = (slice(0, 1), slice(1, 3), slice(3, 5), slice(5, 7), slice(7, 8))
UNITS = 14
PLUS = {1: 0, 2: 1, 3: 3, 4: 5}
MINUS = {1: 0, 2: 2, 3: 4, 4: 6}
ORDER = (
    ("P", 1, 0), ("P", 1, 1), ("P", 0, 0), ("M", 1, 0), ("H", 1, 0), ("Y", 1, 1, 0, 0),
    ("Y", 1, 1, 1, 1), ("P", 1, 2), ("P", 0, 4), ("M", 1, 1), ("Y", 1, 2, 0, 1), ("Y", 1, 2, 1, 0),
    ("M", 0, 0), ("H", 1, 1), ("Y", 0, 1, 0, 0), ("P", 1, 3), ("Y", 0, 1, 1, 1), ("P", 0, 2),
    ("P", 0, 1), ("M", 1, 2), ("P", 0, 3), ("Z", 1, 1, 0, 0), ("Z", 1, 1, 1, 1), ("Y", 1, 2, 1, 1),
    ("H", 0, 0), ("Y", 1, 2, 0, 0), ("H", 1, 2), ("M", 1, 3), ("M", 0, 1), ("Y", 1, 3, 1, 0),
    ("Y", 1, 3, 0, 1), ("P", 1, 4), ("Z", 1, 2, 0, 1), ("M", 1, 4), ("Z", 1, 2, 1, 0),
    ("Z", 1, 2, 1, 1), ("Z", 1, 2, 0, 0), ("M", 0, 2), ("H", 1, 3), ("Y", 1, 3, 0, 0),
    ("Y", 1, 3, 1, 1), ("H", 1, 4), ("Y", 1, 4, 1, 0), ("Y", 1, 4, 0, 1), ("M", 0, 3),
    ("Z", 1, 3, 0, 0), ("Z", 1, 3, 0, 1), ("Z", 1, 3, 1, 0), ("H", 0, 2), ("Z", 1, 3, 1, 1),
    ("Y", 1, 4, 0, 0), ("Y", 1, 4, 1, 1), ("Y", 0, 2, 1, 0), ("H", 0, 1), ("Y", 0, 2, 0, 0),
    ("Z", 1, 4, 0, 0), ("Z", 1, 4, 1, 0), ("Z", 1, 4, 0, 1), ("Z", 1, 4, 1, 1), ("Y", 0, 2, 0, 1),
    ("Z", 0, 1, 0, 0), ("Y", 0, 2, 1, 1), ("Z", 0, 1, 1, 1), ("A", 1), ("Y", 0, 3, 1, 0),
    ("Y", 0, 3, 0, 0), ("B", 1), ("M", 0, 4), ("Z", 0, 2, 0, 1), ("Z", 0, 2, 1, 0), ("H", 0, 3),
    ("Y", 0, 3, 0, 1), ("Z", 0, 2, 0, 0), ("Y", 0, 3, 1, 1), ("Z", 0, 2, 1, 1), ("Y", 0, 4, 0, 0),
    ("H", 0, 4), ("Z", 0, 3, 1, 0), ("Y", 0, 4, 1, 0), ("Y", 0, 4, 0, 1), ("Z", 0, 3, 0, 1),
    ("Y", 0, 4, 1, 1), ("Z", 0, 3, 0, 0), ("Z", 0, 3, 1, 1), ("Z", 0, 4, 1, 0), ("Z", 0, 4, 0, 1),
    ("A", 0), ("Z", 0, 4, 0, 0), ("Z", 0, 4, 1, 1), ("B", 0),
)


def transposed_dot(a, b):
    return lax.dot_general(a, b, (((0,), (0,)), ((), ())), preferred_element_type=jnp.float32)


def head_gradient(query_rows, key_rows, grad_rows, segs):
    length, head = query_rows.shape
    scores = lax.dot_general(
        query_rows, key_rows, (((1,), (1,)), ((), ())), preferred_element_type=jnp.float32
    ) / jnp.sqrt(jnp.float32(head))
    across = jnp.broadcast_to(segs.astype(jnp.float32), (length, length))
    down = across.T
    row = lax.broadcasted_iota(jnp.int32, (length, length), 0)
    column = lax.broadcasted_iota(jnp.int32, (length, length), 1)
    keep = (column <= row) & (across == down)
    masked = jnp.where(keep, scores, jnp.float32(-1e30))
    top = jnp.max(masked, axis=1, keepdims=True)
    weights = jnp.where(keep, jnp.exp(masked - top), jnp.float32(0.0))
    probs = (weights / jnp.sum(weights, axis=1, keepdims=True)).astype(jnp.bfloat16)
    return transposed_dot(probs, grad_rows).astype(jnp.bfloat16)


def kernel(
    split, pipes, acts, queries, keys, grads, segs, out,
    q_buf, k_buf, g_buf, s_buf, a_buf, head_grad,
    part, twin, pair, y_buf, z_buf, y_tail, z_tail, total,
    load_sem, x_send, x_recv, p_send, p_recv, y_send, y_recv, z_send, z_recv, t_send, u_send, t_recv,
    far_sem,
):
    pipe, dp = lax.axis_index("pipe"), lax.axis_index("dp")
    y, low, core = dp // 4, (dp // 2) % 2, dp % 2
    rows = out.shape[0]
    rest = rows - split

    def at(pipe_index, y_index, low_index, core_index):
        return {"pipe": pipe_index, "dp": y_index * 4 + low_index * 2 + core_index}

    twin_id = at(pipe, y, low, 1 - core)
    pair_id = at(pipe, y, 1 - low, core)
    plus_id = at(pipe, (y + 1) % RING, low, core)
    minus_id = at(pipe, (y + RING - 1) % RING, low, core)
    mirror_id = at(pipes - 1 - pipe, y, low, core)
    across_id = at(pipes - 1 - pipe, y, 1 - low, core)
    near = (twin_id, pair_id, plus_id, minus_id)
    distant = (mirror_id, across_id)
    upper = pipe // (pipes // 2)

    barrier = pltpu.get_barrier_semaphore()
    for peer in near:
        pl.semaphore_signal(barrier, inc=1, device_id=peer, device_id_type=MESH)

    @pl.when(upper == 0)
    def _():
        for peer in distant:
            pl.semaphore_signal(barrier, inc=1, device_id=peer, device_id_type=MESH)

    def meet():
        pl.semaphore_wait(barrier, len(near) + len(distant) * upper)

        @pl.when(upper == 1)
        def _():
            for peer in distant:
                pl.semaphore_signal(far_sem, inc=1, device_id=peer, device_id_type=MESH)

    def meet_distant():
        @pl.when(upper == 0)
        def _():
            pl.semaphore_wait(far_sem, len(distant))

    def load(src, dst, number):
        copy = pltpu.make_async_copy(src, dst, load_sem.at[number])
        copy.start()
        return copy

    small = [
        load(src, dst, number)
        for number, (src, dst) in enumerate(
            ((queries, q_buf), (keys, k_buf), (grads, g_buf), (segs, s_buf))
        )
    ]
    wide = 4 * rows
    whole = load(acts, a_buf, 4)
    for copy in small:
        copy.wait()

    def prepare(half):
        head_grad[half] = head_gradient(q_buf[half], k_buf[half], g_buf[half], s_buf[half])

    prepare(1)

    def send(src, dst, send_sem, recv_sem, peer):
        copy = pltpu.make_async_remote_copy(
            src_ref=src, dst_ref=dst, send_sem=send_sem, recv_sem=recv_sem,
            device_id=peer, device_id_type=MESH,
        )
        copy.start()
        return copy

    settled = set()
    exchanges, pairs, y_copies, z_copies, tails = {}, {}, {}, {}, {}
    ways = (plus_id, minus_id)
    last = SLOTS - 1

    def product(half, group):
        for slot in range(SLOTS)[GROUPS[group]]:
            if not exchanges:
                whole.wait()
            first = pl.multiple_of(((y + RING + OFFSETS[slot]) % RING) * wide, 128)
            block = transposed_dot(a_buf[half, :, pl.ds(first, wide)], head_grad[half])
            for z in range(2):
                for c in range(2):
                    start = (z * 2 + c) * rows
                    part[slot, c, half, z] = block[start : start + rows]
        if not exchanges:
            meet()
        slots, number = GROUPS[group], 2 * group + half
        exchanges[half, group] = send(
            part.at[slots, 1 - core, half], twin.at[slots, half],
            x_send, x_recv.at[number], twin_id,
        )

        if len(exchanges) == 1:
            prepare(0)

    def merge(half, group):
        exchanges[half, group].wait_recv()
        for slot in range(SLOTS)[GROUPS[group]]:
            part[slot, core, half] += twin[slot, half]

    def halve(half, group):
        slots, number = GROUPS[group], 2 * group + half
        pairs[half, group] = send(
            part.at[slots, core, half, 1 - low, split:], pair.at[slots, half],
            p_send, p_recv.at[number], pair_id,
        )

    def settle(half, group):
        if (half, group) not in settled:
            settled.add((half, group))
            pairs[half, group].wait_recv()
            for slot in range(SLOTS)[GROUPS[group]]:
                part[slot, core, half, low, split:] += pair[slot, half]

    def z_span(piece):
        return slice(split + piece * (rest // 2), split + (piece + 1) * (rest // 2))

    def place(half, step, way, piece):
        return half * UNITS + (way if step == 1 else 4 * step - 6 + 2 * way + piece)

    def arrive(kind, half, step, way, piece, slot):
        copies = y_copies if kind == "Y" else z_copies
        if (half, step, way, piece) in copies:
            copies[half, step, way, piece].wait_recv()
            if kind == "Y":
                part[slot, core, half, piece, :split] += y_buf[place(half, step, way, piece)]
            else:
                part[slot, core, half, low, z_span(piece)] += z_buf[place(half, step, way, piece)]

    def travel(kind, half, step, way, piece):
        slot = (PLUS, MINUS)[way][step]
        if kind == "Z":
            settle(half, step - 1)
        arrive(kind, half, step - 1, way, piece, slot)
        number = place(half, step, way, piece)
        if kind == "Y":
            y_copies[half, step, way, piece] = send(
                part.at[slot, core, half, piece, :split], y_buf.at[number],
                y_send, y_recv.at[number], ways[way],
            )
        else:
            z_copies[half, step, way, piece] = send(
                part.at[slot, core, half, low, z_span(piece)], z_buf.at[number],
                z_send, z_recv.at[number], ways[way],
            )

    def finish_y(half):
        if half:
            meet_distant()
        for way in range(2):
            for piece in range(2):
                arrive("Y", half, 4, way, piece, last)
        goals = ((1 - low, across_id), (low, mirror_id)) if half else ((1 - low, pair_id),)
        for number, (z, peer) in enumerate(goals, 0 if half else 2):
            tails[number] = send(
                part.at[last, core, half, z, :split], y_tail.at[number],
                t_send, t_recv.at[number], peer,
            )

    def finish_z(half):
        settle(half, len(GROUPS) - 1)
        for way in range(2):
            for piece in range(2):
                arrive("Z", half, 4, way, piece, last)
        if half:
            tails[3] = send(
                part.at[last, core, half, low, split:], z_tail,
                u_send, t_recv.at[3], mirror_id,
            )

    actions = {
        "P": product, "M": merge, "H": halve, "A": finish_y, "B": finish_z,
        "Y": functools.partial(travel, "Y"), "Z": functools.partial(travel, "Z"),
    }
    for action, *values in ORDER:
        actions[action](*values)
    for number in sorted(tails):
        tails[number].wait_recv()
    total[:split] = part[last, core, 0, low, :split] + y_tail[0] + y_tail[1] + y_tail[2]
    total[split:] = part[last, core, 0, low, split:] + z_tail[...]
    out[...] = total[...].astype(out.dtype)
    for landed, sem in (
        (twin, x_send), (pair, p_send), (y_buf, y_send), (z_buf, z_send),
        (y_tail, t_send), (z_tail, u_send),
    ):
        pltpu.make_async_remote_copy(
            src_ref=landed, dst_ref=landed, send_sem=sem, recv_sem=t_recv.at[3],
            device_id=twin_id, device_id_type=MESH,
        ).wait_send()


def body(activations, queries, keys, grad_out, segment_ids):
    _, _, length, width = activations.shape
    head = queries.shape[-1]
    count, pipes = lax.axis_size("dp"), lax.axis_size("pipe")
    rows = width // count
    split = rows * 96 // 192
    rest = rows - split
    f32, bf16 = jnp.float32, jnp.bfloat16
    dma = lambda *shape: pltpu.SemaphoreType.DMA(shape)
    result = pl.pallas_call(
        functools.partial(kernel, split, pipes),
        out_shape=jax.ShapeDtypeStruct((rows, head), bf16),
        in_specs=[pl.BlockSpec(memory_space=pltpu.HBM)] * 5,
        out_specs=pl.BlockSpec(memory_space=pltpu.VMEM),
        scratch_shapes=[
            pltpu.VMEM((2, length, head), bf16),
            pltpu.VMEM((2, length, head), bf16),
            pltpu.VMEM((2, length, head), bf16),
            pltpu.VMEM((2, 1, length), jnp.int32),
            pltpu.VMEM((2, length, width), bf16),
            pltpu.VMEM((2, length, head), bf16),
            pltpu.VMEM((SLOTS, 2, 2, 2, rows, head), f32),
            pltpu.VMEM((SLOTS, 2, 2, rows, head), f32),
            pltpu.VMEM((SLOTS, 2, rest, head), f32),
            pltpu.VMEM((2 * UNITS, split, head), f32),
            pltpu.VMEM((2 * UNITS, rest // 2, head), f32),
            pltpu.VMEM((3, split, head), f32),
            pltpu.VMEM((rest, head), f32),
            pltpu.VMEM((rows, head), f32),
            dma(5), dma(), dma(2 * len(GROUPS)), dma(), dma(2 * len(GROUPS)),
            dma(), dma(2 * UNITS), dma(), dma(2 * UNITS), dma(), dma(), dma(4),
            pltpu.SemaphoreType.REGULAR,
        ],
        compiler_params=pltpu.CompilerParams(
            collective_id=0, has_side_effects=True, vmem_limit_bytes=56_500_000
        ),
        name="reduce_value_grad",
    )(
        activations.reshape(2, length, width),
        queries.reshape(2, length, head),
        keys.reshape(2, length, head),
        grad_out.reshape(2, length, head),
        segment_ids.reshape(2, 1, length),
    )
    return result[None]


def solution(mesh):
    return jax.shard_map(
        body,
        mesh=mesh,
        in_specs=(
            P(None, "pipe", "dp", None),
            P(None, "pipe", "dp", None),
            P(None, "pipe", "dp", None),
            P(None, "pipe", "dp", None),
            P(None, "pipe", "dp", None),
        ),
        out_specs=P("pipe", "dp", None),
        check_vma=False,
    )
```

```python
import functools

import jax
import jax.numpy as jnp
from jax import lax
from jax.experimental import pallas as pl
from jax.experimental.pallas import tpu as pltpu
from jax.sharding import PartitionSpec as P

MESH = pl.DeviceIdType.MESH
RING = 8
OFFSETS = (4, 3, -3, 2, -2, 1, -1, 0)
SLOTS = len(OFFSETS)
GROUPS = (slice(0, 1), slice(1, 3), slice(3, 5), slice(5, 7), slice(7, 8))
UNITS = 14
PLUS = {1: 0, 2: 1, 3: 3, 4: 5}
MINUS = {1: 0, 2: 2, 3: 4, 4: 6}
LOWER_ORDER = (
    ("P", 1, 0), ("P", 1, 1), ("M", 1, 0), ("H", 1, 0), ("Y", 1, 1, 1, 1), ("Y", 1, 1, 0, 0),
    ("P", 0, 0), ("M", 1, 1), ("Y", 1, 2, 1, 0), ("H", 1, 1), ("Y", 1, 2, 0, 1), ("P", 0, 1),
    ("M", 0, 0), ("Y", 0, 1, 1, 1), ("Y", 0, 1, 0, 0), ("H", 0, 0), ("P", 1, 3), ("P", 1, 2),
    ("Z", 1, 1, 1, 1), ("Z", 1, 1, 0, 0), ("M", 0, 1), ("Y", 1, 2, 1, 1), ("M", 1, 3),
    ("Y", 1, 2, 0, 0), ("P", 0, 2), ("M", 1, 2), ("H", 1, 2), ("Y", 1, 3, 1, 0), ("P", 1, 4),
    ("Y", 1, 3, 0, 1), ("H", 0, 1), ("Y", 0, 2, 1, 0), ("Z", 1, 2, 0, 1), ("Z", 1, 2, 1, 0),
    ("Z", 1, 2, 1, 1), ("Z", 1, 2, 0, 0), ("Z", 0, 1, 0, 0), ("M", 1, 4), ("Y", 1, 3, 0, 0),
    ("H", 1, 3), ("Y", 1, 3, 1, 1), ("Y", 0, 2, 0, 1), ("Z", 0, 1, 1, 1), ("M", 0, 2),
    ("Y", 1, 4, 1, 0), ("Z", 1, 3, 0, 1), ("Z", 1, 3, 1, 0), ("Z", 1, 3, 0, 0), ("Y", 1, 4, 0, 1),
    ("Z", 1, 3, 1, 1), ("H", 0, 2), ("Y", 1, 4, 0, 0), ("Y", 0, 2, 0, 0), ("H", 1, 4),
    ("Y", 1, 4, 1, 1), ("P", 0, 4), ("Y", 0, 2, 1, 1), ("Z", 1, 4, 0, 1), ("Z", 1, 4, 0, 0),
    ("Z", 1, 4, 1, 0), ("Z", 1, 4, 1, 1), ("P", 0, 3), ("Z", 0, 2, 1, 1), ("Z", 0, 2, 0, 1),
    ("Y", 0, 3, 1, 0), ("Y", 0, 3, 0, 1), ("A", 1), ("Y", 0, 3, 1, 1), ("Y", 0, 3, 0, 0), ("B", 1),
    ("Z", 0, 2, 0, 0), ("Z", 0, 2, 1, 0), ("M", 0, 4), ("M", 0, 3), ("H", 0, 3), ("Z", 0, 3, 0, 1),
    ("Z", 0, 3, 1, 1), ("Y", 0, 4, 0, 1), ("Y", 0, 4, 1, 0), ("Y", 0, 4, 0, 0), ("Y", 0, 4, 1, 1),
    ("Z", 0, 3, 1, 0), ("H", 0, 4), ("Z", 0, 3, 0, 0), ("Z", 0, 4, 0, 1), ("A", 0),
    ("Z", 0, 4, 1, 1), ("Z", 0, 4, 0, 0), ("Z", 0, 4, 1, 0), ("B", 0),
)
UPPER_ORDER = (
    ("P", 1, 0), ("P", 1, 1), ("M", 1, 0), ("H", 1, 0), ("Y", 1, 1, 1, 1), ("Y", 1, 1, 0, 0),
    ("P", 1, 4), ("P", 0, 0), ("M", 1, 1), ("Y", 1, 2, 1, 0), ("H", 1, 1), ("Y", 1, 2, 0, 1),
    ("P", 1, 2), ("M", 0, 0), ("M", 1, 4), ("Y", 0, 1, 1, 1), ("Y", 0, 1, 0, 0), ("P", 0, 2),
    ("P", 0, 4), ("H", 1, 4), ("M", 1, 2), ("Z", 1, 1, 0, 0), ("Z", 1, 1, 1, 1), ("H", 0, 0),
    ("Y", 1, 2, 0, 0), ("Y", 1, 2, 1, 1), ("P", 0, 1), ("P", 1, 3), ("Y", 1, 3, 1, 0), ("H", 1, 2),
    ("Y", 1, 3, 0, 1), ("M", 0, 2), ("Z", 1, 2, 1, 0), ("M", 1, 3), ("M", 0, 4), ("Z", 1, 2, 0, 0),
    ("Z", 1, 2, 1, 1), ("H", 1, 3), ("Z", 1, 2, 0, 1), ("M", 0, 1), ("P", 0, 3), ("H", 0, 1),
    ("Y", 1, 3, 0, 0), ("Y", 1, 3, 1, 1), ("H", 0, 2), ("Z", 0, 1, 0, 0), ("Y", 1, 4, 0, 1),
    ("Y", 1, 4, 1, 0), ("Z", 1, 3, 1, 1), ("Z", 1, 3, 0, 0), ("M", 0, 3), ("Z", 1, 3, 0, 1),
    ("Z", 1, 3, 1, 0), ("Y", 1, 4, 0, 0), ("Y", 1, 4, 1, 1), ("Y", 0, 2, 0, 0), ("Y", 0, 2, 1, 0),
    ("Z", 1, 4, 0, 0), ("Z", 1, 4, 1, 1), ("Z", 1, 4, 1, 0), ("Z", 1, 4, 0, 1), ("Y", 0, 2, 0, 1),
    ("Y", 0, 2, 1, 1), ("Z", 0, 2, 0, 1), ("A", 1), ("Z", 0, 2, 0, 0), ("Z", 0, 2, 1, 0),
    ("Z", 0, 1, 1, 1), ("Y", 0, 3, 1, 0), ("Y", 0, 3, 0, 0), ("B", 1), ("Y", 0, 3, 1, 1),
    ("Y", 0, 3, 0, 1), ("Z", 0, 3, 0, 0), ("Z", 0, 3, 0, 1), ("H", 0, 3), ("Z", 0, 2, 1, 1),
    ("Z", 0, 3, 1, 0), ("Y", 0, 4, 1, 0), ("Y", 0, 4, 0, 0), ("Y", 0, 4, 1, 1), ("Y", 0, 4, 0, 1),
    ("Z", 0, 3, 1, 1), ("Z", 0, 4, 0, 1), ("Z", 0, 4, 1, 0), ("Z", 0, 4, 0, 0), ("H", 0, 4),
    ("A", 0), ("Z", 0, 4, 1, 1), ("B", 0),
)


def transposed_dot(a, b):
    return lax.dot_general(a, b, (((0,), (0,)), ((), ())), preferred_element_type=jnp.float32)


def head_gradient(query_rows, key_rows, grad_rows, segs):
    length, head = query_rows.shape
    scores = lax.dot_general(
        query_rows, key_rows, (((1,), (1,)), ((), ())), preferred_element_type=jnp.float32
    ) / jnp.sqrt(jnp.float32(head))
    across = jnp.broadcast_to(segs.astype(jnp.float32), (length, length))
    down = across.T
    row = lax.broadcasted_iota(jnp.int32, (length, length), 0)
    column = lax.broadcasted_iota(jnp.int32, (length, length), 1)
    keep = (column <= row) & (across == down)
    masked = jnp.where(keep, scores, jnp.float32(-1e30))
    top = jnp.max(masked, axis=1, keepdims=True)
    weights = jnp.where(keep, jnp.exp(masked - top), jnp.float32(0.0))
    probs = (weights / jnp.sum(weights, axis=1, keepdims=True)).astype(jnp.bfloat16)
    return transposed_dot(probs, grad_rows).astype(jnp.bfloat16)


def kernel(
    split, pipes, acts, queries, keys, grads, segs, out,
    q_buf, k_buf, g_buf, s_buf, a_buf, head_grad,
    part, twin, pair, y_buf, z_buf, y_tail, z_tail, total,
    load_sem, x_send, x_recv, p_send, p_recv, y_send, y_recv, z_send, z_recv, t_send, u_send, t_recv,
    far_sem,
):
    pipe, dp = lax.axis_index("pipe"), lax.axis_index("dp")
    y, low, core = dp // 4, (dp // 2) % 2, dp % 2
    rows = out.shape[0]
    rest = rows - split

    def at(pipe_index, y_index, low_index, core_index):
        return {"pipe": pipe_index, "dp": y_index * 4 + low_index * 2 + core_index}

    twin_id = at(pipe, y, low, 1 - core)
    pair_id = at(pipe, y, 1 - low, core)
    plus_id = at(pipe, (y + 1) % RING, low, core)
    minus_id = at(pipe, (y + RING - 1) % RING, low, core)
    mirror_id = at(pipes - 1 - pipe, y, low, core)
    across_id = at(pipes - 1 - pipe, y, 1 - low, core)
    near = (twin_id, pair_id, plus_id, minus_id)
    distant = (mirror_id, across_id)
    upper = pipe // (pipes // 2)

    barrier = pltpu.get_barrier_semaphore()
    for peer in near:
        pl.semaphore_signal(barrier, inc=1, device_id=peer, device_id_type=MESH)

    @pl.when(upper == 0)
    def _():
        for peer in distant:
            pl.semaphore_signal(barrier, inc=1, device_id=peer, device_id_type=MESH)

    def meet():
        pl.semaphore_wait(barrier, len(near) + len(distant) * upper)

        @pl.when(upper == 1)
        def _():
            for peer in distant:
                pl.semaphore_signal(far_sem, inc=1, device_id=peer, device_id_type=MESH)

    def meet_distant():
        @pl.when(upper == 0)
        def _():
            pl.semaphore_wait(far_sem, len(distant))

    def load(src, dst, number):
        copy = pltpu.make_async_copy(src, dst, load_sem.at[number])
        copy.start()
        return copy

    small = [
        load(src, dst, number)
        for number, (src, dst) in enumerate(
            ((queries, q_buf), (keys, k_buf), (grads, g_buf), (segs, s_buf))
        )
    ]
    wide = 4 * rows
    large = []
    for slot, offset in enumerate(OFFSETS):
        first = pl.multiple_of(((y + RING + offset) % RING) * wide, 128)
        large.append(
            pltpu.make_async_copy(
                acts.at[:, :, pl.ds(first, wide)], a_buf.at[slot], load_sem.at[4 + slot]
            )
        )
    large[0].start()
    for copy in small:
        copy.wait()

    def prepare(half):
        head_grad[half] = head_gradient(q_buf[half], k_buf[half], g_buf[half], s_buf[half])

    prepare(1)
    for copy in large[1:]:
        copy.start()

    def send(src, dst, send_sem, recv_sem, peer):
        copy = pltpu.make_async_remote_copy(
            src_ref=src, dst_ref=dst, send_sem=send_sem, recv_sem=recv_sem,
            device_id=peer, device_id_type=MESH,
        )
        copy.start()
        return copy

    loaded, settled = set(), set()
    exchanges, pairs, y_copies, z_copies, tails = {}, {}, {}, {}, {}
    records = (loaded, settled, exchanges, pairs, y_copies, z_copies, tails)
    ways = (plus_id, minus_id)
    last = SLOTS - 1

    def product(half, group):
        for slot in range(SLOTS)[GROUPS[group]]:
            if slot not in loaded:
                loaded.add(slot)
                large[slot].wait()
            block = transposed_dot(a_buf[slot, half], head_grad[half])
            for z in range(2):
                for c in range(2):
                    start = (z * 2 + c) * rows
                    part[slot, c, half, z] = block[start : start + rows]
        if not exchanges:
            meet()
        slots, number = GROUPS[group], 2 * group + half
        exchanges[half, group] = send(
            part.at[slots, 1 - core, half], twin.at[slots, half],
            x_send, x_recv.at[number], twin_id,
        )

        if len(exchanges) == 1:
            prepare(0)

    def merge(half, group):
        exchanges[half, group].wait_recv()
        for slot in range(SLOTS)[GROUPS[group]]:
            part[slot, core, half] += twin[slot, half]

    def halve(half, group):
        slots, number = GROUPS[group], 2 * group + half
        pairs[half, group] = send(
            part.at[slots, core, half, 1 - low, split:], pair.at[slots, half],
            p_send, p_recv.at[number], pair_id,
        )

    def settle(half, group):
        if (half, group) not in settled:
            settled.add((half, group))
            pairs[half, group].wait_recv()
            for slot in range(SLOTS)[GROUPS[group]]:
                part[slot, core, half, low, split:] += pair[slot, half]

    def z_span(piece):
        return slice(split + piece * (rest // 2), split + (piece + 1) * (rest // 2))

    def place(half, step, way, piece):
        return half * UNITS + (way if step == 1 else 4 * step - 6 + 2 * way + piece)

    def arrive(kind, half, step, way, piece, slot):
        copies = y_copies if kind == "Y" else z_copies
        if (half, step, way, piece) in copies:
            copies[half, step, way, piece].wait_recv()
            if kind == "Y":
                part[slot, core, half, piece, :split] += y_buf[place(half, step, way, piece)]
            else:
                part[slot, core, half, low, z_span(piece)] += z_buf[place(half, step, way, piece)]

    def travel(kind, half, step, way, piece):
        slot = (PLUS, MINUS)[way][step]
        if kind == "Z":
            settle(half, step - 1)
        arrive(kind, half, step - 1, way, piece, slot)
        number = place(half, step, way, piece)
        if kind == "Y":
            y_copies[half, step, way, piece] = send(
                part.at[slot, core, half, piece, :split], y_buf.at[number],
                y_send, y_recv.at[number], ways[way],
            )
        else:
            z_copies[half, step, way, piece] = send(
                part.at[slot, core, half, low, z_span(piece)], z_buf.at[number],
                z_send, z_recv.at[number], ways[way],
            )

    def finish_y(half):
        if half and not tails:
            meet_distant()
        for way in range(2):
            for piece in range(2):
                arrive("Y", half, 4, way, piece, last)
        goals = ((1 - low, across_id), (low, mirror_id)) if half else ((1 - low, pair_id),)
        for number, (z, peer) in enumerate(goals, 0 if half else 2):
            tails[number] = send(
                part.at[last, core, half, z, :split], y_tail.at[number],
                t_send, t_recv.at[number], peer,
            )

    def finish_z(half):
        settle(half, len(GROUPS) - 1)
        for way in range(2):
            for piece in range(2):
                arrive("Z", half, 4, way, piece, last)
        if half:
            if not tails:
                meet_distant()
            tails[3] = send(
                part.at[last, core, half, low, split:], z_tail,
                u_send, t_recv.at[3], mirror_id,
            )

    actions = {
        "P": product, "M": merge, "H": halve, "A": finish_y, "B": finish_z,
        "Y": functools.partial(travel, "Y"), "Z": functools.partial(travel, "Z"),
    }

    for side, order in enumerate((LOWER_ORDER, UPPER_ORDER)):

        @pl.when(upper == side)
        def _():
            for record in records:
                record.clear()
            for action, *values in order:
                actions[action](*values)
            for number in sorted(tails):
                tails[number].wait_recv()

    total[:split] = part[last, core, 0, low, :split] + y_tail[0] + y_tail[1] + y_tail[2]
    total[split:] = part[last, core, 0, low, split:] + z_tail[...]
    out[...] = total[...].astype(out.dtype)
    for landed, sem in (
        (twin, x_send), (pair, p_send), (y_buf, y_send), (z_buf, z_send),
        (y_tail, t_send), (z_tail, u_send),
    ):
        pltpu.make_async_remote_copy(
            src_ref=landed, dst_ref=landed, send_sem=sem, recv_sem=t_recv.at[3],
            device_id=twin_id, device_id_type=MESH,
        ).wait_send()


def body(activations, queries, keys, grad_out, segment_ids):
    _, _, length, width = activations.shape
    head = queries.shape[-1]
    count, pipes = lax.axis_size("dp"), lax.axis_size("pipe")
    rows = width // count
    split = rows // 2
    rest = rows - split
    f32, bf16 = jnp.float32, jnp.bfloat16
    dma = lambda *shape: pltpu.SemaphoreType.DMA(shape)
    result = pl.pallas_call(
        functools.partial(kernel, split, pipes),
        out_shape=jax.ShapeDtypeStruct((rows, head), bf16),
        in_specs=[pl.BlockSpec(memory_space=pltpu.HBM)] * 5,
        out_specs=pl.BlockSpec(memory_space=pltpu.VMEM),
        scratch_shapes=[
            pltpu.VMEM((2, length, head), bf16),
            pltpu.VMEM((2, length, head), bf16),
            pltpu.VMEM((2, length, head), bf16),
            pltpu.VMEM((2, 1, length), jnp.int32),
            pltpu.VMEM((SLOTS, 2, length, 4 * rows), bf16),
            pltpu.VMEM((2, length, head), bf16),
            pltpu.VMEM((SLOTS, 2, 2, 2, rows, head), f32),
            pltpu.VMEM((SLOTS, 2, 2, rows, head), f32),
            pltpu.VMEM((SLOTS, 2, rest, head), f32),
            pltpu.VMEM((2 * UNITS, split, head), f32),
            pltpu.VMEM((2 * UNITS, rest // 2, head), f32),
            pltpu.VMEM((3, split, head), f32),
            pltpu.VMEM((rest, head), f32),
            pltpu.VMEM((rows, head), f32),
            dma(4 + SLOTS), dma(), dma(2 * len(GROUPS)), dma(), dma(2 * len(GROUPS)),
            dma(), dma(2 * UNITS), dma(), dma(2 * UNITS), dma(), dma(), dma(4),
            pltpu.SemaphoreType.REGULAR,
        ],
        compiler_params=pltpu.CompilerParams(
            collective_id=0, has_side_effects=True, vmem_limit_bytes=48 * 2**20
        ),
        name="reduce_value_grad",
    )(
        *(
            pltpu.with_memory_space_constraint(operand, pltpu.HBM)
            for operand in (
                activations.reshape(2, length, width),
                queries.reshape(2, length, head),
                keys.reshape(2, length, head),
                grad_out.reshape(2, length, head),
                segment_ids.reshape(2, 1, length),
            )
        )
    )
    return result[None]


def solution(mesh):
    return jax.shard_map(
        body,
        mesh=mesh,
        in_specs=(
            P(None, "pipe", "dp", None),
            P(None, "pipe", "dp", None),
            P(None, "pipe", "dp", None),
            P(None, "pipe", "dp", None),
            P(None, "pipe", "dp", None),
        ),
        out_specs=P("pipe", "dp", None),
        check_vma=False,
    )
```

```python
import functools

import jax
import jax.numpy as jnp
from jax import lax
from jax.experimental import pallas as pl
from jax.experimental.pallas import tpu as pltpu
from jax.sharding import PartitionSpec as P

MESH = pl.DeviceIdType.MESH
RING = 8
OFFSETS = (4, 3, -3, 2, -2, 1, -1, 0)
SLOTS = len(OFFSETS)
GROUPS = (slice(0, 1), slice(1, 3), slice(3, 5), slice(5, 7), slice(7, 8))
UNITS = 14
PLUS = {1: 0, 2: 1, 3: 3, 4: 5}
MINUS = {1: 0, 2: 2, 3: 4, 4: 6}
LOWER_ORDER = (
    ("P", 1, 0), ("P", 1, 1), ("M", 1, 0), ("H", 1, 0), ("Y", 1, 1, 1, 1), ("Y", 1, 1, 0, 0),
    ("P", 0, 0), ("M", 1, 1), ("Y", 1, 2, 1, 0), ("H", 1, 1), ("Y", 1, 2, 0, 1), ("P", 0, 1),
    ("M", 0, 0), ("Y", 0, 1, 1, 1), ("Y", 0, 1, 0, 0), ("H", 0, 0), ("P", 1, 3), ("P", 1, 2),
    ("Z", 1, 1, 1, 1), ("Z", 1, 1, 0, 0), ("M", 0, 1), ("Y", 1, 2, 1, 1), ("M", 1, 3),
    ("Y", 1, 2, 0, 0), ("P", 0, 2), ("M", 1, 2), ("H", 1, 2), ("Y", 1, 3, 1, 0), ("P", 1, 4),
    ("Y", 1, 3, 0, 1), ("H", 0, 1), ("Y", 0, 2, 1, 0), ("Z", 1, 2, 0, 1), ("Z", 1, 2, 1, 0),
    ("Z", 1, 2, 1, 1), ("Z", 1, 2, 0, 0), ("Z", 0, 1, 0, 0), ("M", 1, 4), ("Y", 1, 3, 0, 0),
    ("H", 1, 3), ("Y", 1, 3, 1, 1), ("Y", 0, 2, 0, 1), ("Z", 0, 1, 1, 1), ("M", 0, 2),
    ("Y", 1, 4, 1, 0), ("Z", 1, 3, 0, 1), ("Z", 1, 3, 1, 0), ("Z", 1, 3, 0, 0), ("Y", 1, 4, 0, 1),
    ("Z", 1, 3, 1, 1), ("H", 0, 2), ("Y", 1, 4, 0, 0), ("Y", 0, 2, 0, 0), ("H", 1, 4),
    ("Y", 1, 4, 1, 1), ("P", 0, 4), ("Y", 0, 2, 1, 1), ("Z", 1, 4, 0, 1), ("Z", 1, 4, 0, 0),
    ("Z", 1, 4, 1, 0), ("Z", 1, 4, 1, 1), ("P", 0, 3), ("Z", 0, 2, 1, 1), ("Z", 0, 2, 0, 1),
    ("Y", 0, 3, 1, 0), ("Y", 0, 3, 0, 1), ("A", 1), ("Y", 0, 3, 1, 1), ("Y", 0, 3, 0, 0), ("B", 1),
    ("Z", 0, 2, 0, 0), ("Z", 0, 2, 1, 0), ("M", 0, 4), ("M", 0, 3), ("H", 0, 3), ("Z", 0, 3, 0, 1),
    ("Z", 0, 3, 1, 1), ("Y", 0, 4, 0, 1), ("Y", 0, 4, 1, 0), ("Y", 0, 4, 0, 0), ("Y", 0, 4, 1, 1),
    ("Z", 0, 3, 1, 0), ("H", 0, 4), ("Z", 0, 3, 0, 0), ("Z", 0, 4, 0, 1), ("A", 0),
    ("Z", 0, 4, 1, 1), ("Z", 0, 4, 0, 0), ("Z", 0, 4, 1, 0), ("B", 0),
)
UPPER_ORDER = (
    ("P", 1, 0), ("P", 1, 1), ("M", 1, 0), ("H", 1, 0), ("Y", 1, 1, 1, 1), ("Y", 1, 1, 0, 0),
    ("P", 1, 4), ("P", 0, 0), ("M", 1, 1), ("Y", 1, 2, 1, 0), ("H", 1, 1), ("Y", 1, 2, 0, 1),
    ("P", 1, 2), ("M", 0, 0), ("M", 1, 4), ("Y", 0, 1, 1, 1), ("Y", 0, 1, 0, 0), ("P", 0, 2),
    ("P", 0, 4), ("H", 1, 4), ("M", 1, 2), ("Z", 1, 1, 0, 0), ("Z", 1, 1, 1, 1), ("H", 0, 0),
    ("Y", 1, 2, 0, 0), ("Y", 1, 2, 1, 1), ("P", 0, 1), ("P", 1, 3), ("Y", 1, 3, 1, 0), ("H", 1, 2),
    ("Y", 1, 3, 0, 1), ("M", 0, 2), ("Z", 1, 2, 1, 0), ("M", 1, 3), ("M", 0, 4), ("Z", 1, 2, 0, 0),
    ("Z", 1, 2, 1, 1), ("H", 1, 3), ("Z", 1, 2, 0, 1), ("M", 0, 1), ("P", 0, 3), ("H", 0, 1),
    ("Y", 1, 3, 0, 0), ("Y", 1, 3, 1, 1), ("H", 0, 2), ("Z", 0, 1, 0, 0), ("Y", 1, 4, 0, 1),
    ("Y", 1, 4, 1, 0), ("Z", 1, 3, 1, 1), ("Z", 1, 3, 0, 0), ("M", 0, 3), ("Z", 1, 3, 0, 1),
    ("Z", 1, 3, 1, 0), ("Y", 1, 4, 0, 0), ("Y", 1, 4, 1, 1), ("Y", 0, 2, 0, 0), ("Y", 0, 2, 1, 0),
    ("Z", 1, 4, 0, 0), ("Z", 1, 4, 1, 1), ("Z", 1, 4, 1, 0), ("Z", 1, 4, 0, 1), ("Y", 0, 2, 0, 1),
    ("Y", 0, 2, 1, 1), ("Z", 0, 2, 0, 1), ("A", 1), ("Z", 0, 2, 0, 0), ("Z", 0, 2, 1, 0),
    ("Z", 0, 1, 1, 1), ("Y", 0, 3, 1, 0), ("Y", 0, 3, 0, 0), ("B", 1), ("Y", 0, 3, 1, 1),
    ("Y", 0, 3, 0, 1), ("Z", 0, 3, 0, 0), ("Z", 0, 3, 0, 1), ("H", 0, 3), ("Z", 0, 2, 1, 1),
    ("Z", 0, 3, 1, 0), ("Y", 0, 4, 1, 0), ("Y", 0, 4, 0, 0), ("Y", 0, 4, 1, 1), ("Y", 0, 4, 0, 1),
    ("Z", 0, 3, 1, 1), ("Z", 0, 4, 0, 1), ("Z", 0, 4, 1, 0), ("Z", 0, 4, 0, 0), ("H", 0, 4),
    ("A", 0), ("Z", 0, 4, 1, 1), ("B", 0),
)


def transposed_dot(a, b):
    return lax.dot_general(a, b, (((0,), (0,)), ((), ())), preferred_element_type=jnp.float32)


def head_gradient(query_rows, key_rows, grad_rows, segs):
    length, head = query_rows.shape
    scores = lax.dot_general(
        query_rows, key_rows, (((1,), (1,)), ((), ())), preferred_element_type=jnp.float32
    ) / jnp.sqrt(jnp.float32(head))
    across = jnp.broadcast_to(segs.astype(jnp.float32), (length, length))
    down = across.T
    row = lax.broadcasted_iota(jnp.int32, (length, length), 0)
    column = lax.broadcasted_iota(jnp.int32, (length, length), 1)
    keep = (column <= row) & (across == down)
    masked = jnp.where(keep, scores, jnp.float32(-1e30))
    top = jnp.max(masked, axis=1, keepdims=True)
    weights = jnp.where(keep, jnp.exp(masked - top), jnp.float32(0.0))
    probs = (weights / jnp.sum(weights, axis=1, keepdims=True)).astype(jnp.bfloat16)
    return transposed_dot(probs, grad_rows).astype(jnp.bfloat16)


def kernel(
    split, pipes, acts, queries, keys, grads, segs, out,
    q_buf, k_buf, g_buf, s_buf, a_buf, head_grad,
    part, twin, pair, y_buf, z_buf, y_tail, z_tail, total,
    load_sem, x_send, x_recv, p_send, p_recv, y_send, y_recv, z_send, z_recv, t_send, u_send, t_recv,
    far_sem,
):
    pipe, dp = lax.axis_index("pipe"), lax.axis_index("dp")
    y, low, core = dp // 4, (dp // 2) % 2, dp % 2
    rows = out.shape[0]
    rest = rows - split

    def at(pipe_index, y_index, low_index, core_index):
        return {"pipe": pipe_index, "dp": y_index * 4 + low_index * 2 + core_index}

    twin_id = at(pipe, y, low, 1 - core)
    pair_id = at(pipe, y, 1 - low, core)
    plus_id = at(pipe, (y + 1) % RING, low, core)
    minus_id = at(pipe, (y + RING - 1) % RING, low, core)
    mirror_id = at(pipes - 1 - pipe, y, low, core)
    across_id = at(pipes - 1 - pipe, y, 1 - low, core)
    near = (twin_id, pair_id, plus_id, minus_id)
    distant = (mirror_id, across_id)
    upper = pipe // (pipes // 2)

    barrier = pltpu.get_barrier_semaphore()
    for peer in near:
        pl.semaphore_signal(barrier, inc=1, device_id=peer, device_id_type=MESH)

    @pl.when(upper == 0)
    def _():
        for peer in distant:
            pl.semaphore_signal(barrier, inc=1, device_id=peer, device_id_type=MESH)

    def meet():
        pl.semaphore_wait(barrier, len(near) + len(distant) * upper)

        @pl.when(upper == 1)
        def _():
            for peer in distant:
                pl.semaphore_signal(far_sem, inc=1, device_id=peer, device_id_type=MESH)

    def meet_distant():
        @pl.when(upper == 0)
        def _():
            pl.semaphore_wait(far_sem, len(distant))

    def load(src, dst, number):
        copy = pltpu.make_async_copy(src, dst, load_sem.at[number])
        copy.start()
        return copy

    small = [
        load(src, dst, number)
        for number, (src, dst) in enumerate(
            ((queries, q_buf), (keys, k_buf), (grads, g_buf), (segs, s_buf))
        )
    ]
    wide = 4 * rows
    large = []
    for slot, offset in enumerate(OFFSETS):
        first = pl.multiple_of(((y + RING + offset) % RING) * wide, 128)
        large.append(
            pltpu.make_async_copy(
                acts.at[:, :, pl.ds(first, wide)], a_buf.at[slot], load_sem.at[4 + slot]
            )
        )
    large[0].start()
    for copy in small:
        copy.wait()

    def prepare(half):
        head_grad[half] = head_gradient(q_buf[half], k_buf[half], g_buf[half], s_buf[half])

    prepare(1)
    for copy in large[1:]:
        copy.start()

    def send(src, dst, send_sem, recv_sem, peer):
        copy = pltpu.make_async_remote_copy(
            src_ref=src, dst_ref=dst, send_sem=send_sem, recv_sem=recv_sem,
            device_id=peer, device_id_type=MESH,
        )
        copy.start()
        return copy

    loaded, settled = set(), set()
    exchanges, pairs, y_copies, z_copies, tails = {}, {}, {}, {}, {}
    records = (loaded, settled, exchanges, pairs, y_copies, z_copies, tails)
    ways = (plus_id, minus_id)
    last = SLOTS - 1

    def product(half, group):
        for slot in range(SLOTS)[GROUPS[group]]:
            if slot not in loaded:
                loaded.add(slot)
                large[slot].wait()
            block = transposed_dot(a_buf[slot, half], head_grad[half])
            for z in range(2):
                for c in range(2):
                    start = (z * 2 + c) * rows
                    part[slot, c, half, z] = block[start : start + rows]
        if not exchanges:
            meet()
        slots, number = GROUPS[group], 2 * group + half
        exchanges[half, group] = send(
            part.at[slots, 1 - core, half], twin.at[slots, half],
            x_send, x_recv.at[number], twin_id,
        )

        if len(exchanges) == 1:
            prepare(0)

    def merge(half, group):
        exchanges[half, group].wait_recv()
        for slot in range(SLOTS)[GROUPS[group]]:
            part[slot, core, half] += twin[slot, half]

    def halve(half, group):
        slots, number = GROUPS[group], 2 * group + half
        pairs[half, group] = send(
            part.at[slots, core, half, 1 - low, split:], pair.at[slots, half],
            p_send, p_recv.at[number], pair_id,
        )

    def settle(half, group):
        if (half, group) not in settled:
            settled.add((half, group))
            pairs[half, group].wait_recv()
            for slot in range(SLOTS)[GROUPS[group]]:
                part[slot, core, half, low, split:] += pair[slot, half]

    def z_span(piece):
        return slice(split + piece * (rest // 2), split + (piece + 1) * (rest // 2))

    def place(half, step, way, piece):
        return half * UNITS + (way if step == 1 else 4 * step - 6 + 2 * way + piece)

    def arrive(kind, half, step, way, piece, slot):
        copies = y_copies if kind == "Y" else z_copies
        if (half, step, way, piece) in copies:
            copies[half, step, way, piece].wait_recv()
            if kind == "Y":
                part[slot, core, half, piece, :split] += y_buf[place(half, step, way, piece)]
            else:
                part[slot, core, half, low, z_span(piece)] += z_buf[place(half, step, way, piece)]

    def travel(kind, half, step, way, piece):
        slot = (PLUS, MINUS)[way][step]
        if kind == "Z":
            settle(half, step - 1)
        arrive(kind, half, step - 1, way, piece, slot)
        number = place(half, step, way, piece)
        if kind == "Y":
            y_copies[half, step, way, piece] = send(
                part.at[slot, core, half, piece, :split], y_buf.at[number],
                y_send, y_recv.at[number], ways[way],
            )
        else:
            z_copies[half, step, way, piece] = send(
                part.at[slot, core, half, low, z_span(piece)], z_buf.at[number],
                z_send, z_recv.at[number], ways[way],
            )

    def finish_y(half):
        if half and not tails:
            meet_distant()
        for way in range(2):
            for piece in range(2):
                arrive("Y", half, 4, way, piece, last)
        goals = ((1 - low, across_id), (low, mirror_id)) if half else ((1 - low, pair_id),)
        for number, (z, peer) in enumerate(goals, 0 if half else 2):
            tails[number] = send(
                part.at[last, core, half, z, :split], y_tail.at[number],
                t_send, t_recv.at[number], peer,
            )

    def finish_z(half):
        settle(half, len(GROUPS) - 1)
        for way in range(2):
            for piece in range(2):
                arrive("Z", half, 4, way, piece, last)
        if half:
            if not tails:
                meet_distant()
            tails[3] = send(
                part.at[last, core, half, low, split:], z_tail,
                u_send, t_recv.at[3], mirror_id,
            )

    actions = {
        "P": product, "M": merge, "H": halve, "A": finish_y, "B": finish_z,
        "Y": functools.partial(travel, "Y"), "Z": functools.partial(travel, "Z"),
    }

    for side, order in enumerate((LOWER_ORDER, UPPER_ORDER)):

        @pl.when(upper == side)
        def _():
            for record in records:
                record.clear()
            for action, *values in order:
                actions[action](*values)
            for number in sorted(tails):
                tails[number].wait_recv()

    total[:split] = part[last, core, 0, low, :split] + y_tail[0] + y_tail[1] + y_tail[2]
    total[split:] = part[last, core, 0, low, split:] + z_tail[...]
    out[...] = total[...].astype(out.dtype)
    for landed, sem in (
        (twin, x_send), (pair, p_send), (y_buf, y_send), (z_buf, z_send),
        (y_tail, t_send), (z_tail, u_send),
    ):
        pltpu.make_async_remote_copy(
            src_ref=landed, dst_ref=landed, send_sem=sem, recv_sem=t_recv.at[3],
            device_id=twin_id, device_id_type=MESH,
        ).wait_send()


def body(activations, queries, keys, grad_out, segment_ids):
    _, _, length, width = activations.shape
    head = queries.shape[-1]
    count, pipes = lax.axis_size("dp"), lax.axis_size("pipe")
    rows = width // count
    split = rows * 80 // 192
    rest = rows - split
    f32, bf16 = jnp.float32, jnp.bfloat16
    dma = lambda *shape: pltpu.SemaphoreType.DMA(shape)
    result = pl.pallas_call(
        functools.partial(kernel, split, pipes),
        out_shape=jax.ShapeDtypeStruct((rows, head), bf16),
        in_specs=[pl.BlockSpec(memory_space=pltpu.HBM)] * 5,
        out_specs=pl.BlockSpec(memory_space=pltpu.VMEM),
        scratch_shapes=[
            pltpu.VMEM((2, length, head), bf16),
            pltpu.VMEM((2, length, head), bf16),
            pltpu.VMEM((2, length, head), bf16),
            pltpu.VMEM((2, 1, length), jnp.int32),
            pltpu.VMEM((SLOTS, 2, length, 4 * rows), bf16),
            pltpu.VMEM((2, length, head), bf16),
            pltpu.VMEM((SLOTS, 2, 2, 2, rows, head), f32),
            pltpu.VMEM((SLOTS, 2, 2, rows, head), f32),
            pltpu.VMEM((SLOTS, 2, rest, head), f32),
            pltpu.VMEM((2 * UNITS, split, head), f32),
            pltpu.VMEM((2 * UNITS, rest // 2, head), f32),
            pltpu.VMEM((3, split, head), f32),
            pltpu.VMEM((rest, head), f32),
            pltpu.VMEM((rows, head), f32),
            dma(4 + SLOTS), dma(), dma(2 * len(GROUPS)), dma(), dma(2 * len(GROUPS)),
            dma(), dma(2 * UNITS), dma(), dma(2 * UNITS), dma(), dma(), dma(4),
            pltpu.SemaphoreType.REGULAR,
        ],
        compiler_params=pltpu.CompilerParams(
            collective_id=0, has_side_effects=True, vmem_limit_bytes=48 * 2**20
        ),
        name="reduce_value_grad",
    )(
        *(
            pltpu.with_memory_space_constraint(operand, pltpu.HBM)
            for operand in (
                activations.reshape(2, length, width),
                queries.reshape(2, length, head),
                keys.reshape(2, length, head),
                grad_out.reshape(2, length, head),
                segment_ids.reshape(2, 1, length),
            )
        )
    )
    return result[None]


def solution(mesh):
    return jax.shard_map(
        body,
        mesh=mesh,
        in_specs=(
            P(None, "pipe", "dp", None),
            P(None, "pipe", "dp", None),
            P(None, "pipe", "dp", None),
            P(None, "pipe", "dp", None),
            P(None, "pipe", "dp", None),
        ),
        out_specs=P("pipe", "dp", None),
        check_vma=False,
    )
```
